32 devices in a mesh: gx: 4 (over x, core), gy: 2 (over y), gz: 4 (over z).
Axes of the slice: x: 2, y: 2, z: 4, core: 2. Of those that a mesh axis runs over, the one named last changes fastest.
Arguments:
- hamiltonian: float32 [4, 2, 4, 7, 384, 384], P('gx', 'gy', 'gz'), may hold values from -20 to 20, as said below
- keep_mask: int32 [4, 2, 4, 7], P('gx', 'gy', 'gz'), may hold values from 0 to 1, as said below
Outputs:
- sign_blocks: float32 [4, 2, 4, 7, 384, 384], P('gx', 'gy', 'gz')
The draws below stay inside these ranges and needn't reach their ends.
Inputs may be any that keep to these rules, and one draw needn't show every extreme that they name: `hamiltonian`: entries are real numbers; the blocks are dense. `keep_mask`: slot 0 is 1 for every domain.
All inputs are finite; a program needn't handle non-finite values.
Results may differ from the reference program's by a relative error of at most 0.00025.
Values sent between devices are 32-bit elements; how exact they have to be, the bound alone decides.
No kernel may reach another device: no remote copies, remote signals or barrier semaphores. Data moves between devices by JAX's collectives and lax.ppermute only.
A program may use at most 128 MiB of HBM per device.

```python
import math
import jax
import jax.numpy as jnp
from jax import lax

B = 384
ITERS = 1
NX = 4
NY = 2
NZ = 4


def draw_hamiltonian(key, part):
    keys = jax.random.split(key, 5)
    shape = (NX, NY, NZ, 7, B, B)
    noise = jax.random.normal(keys[0], shape, jnp.float32)
    signs = jax.random.randint(keys[1], (NX, NY, NZ, B), 0, 2).astype(jnp.float32) * 2.0 - 1.0
    magnitude = jax.random.uniform(keys[2], (NX, NY, NZ, B), jnp.float32, 0.2, 0.6)
    onsite = signs * magnitude
    identity = jnp.eye(B, dtype=jnp.float32)
    first_slot = (jnp.arange(7) == 0).astype(jnp.float32)
    matrix = 0.02 * noise + first_slot[:, None, None] * identity * onsite[:, :, :, None, None, :]
    row_scale = jnp.exp(jax.random.uniform(keys[3], (NX, NY, NZ, 1, B, 1), jnp.float32, 0.0, 0.5 * math.log(10.0)))
    col_scale = jnp.exp(jax.random.uniform(keys[4], (NX, NY, NZ, 7, 1, B), jnp.float32, 0.0, 0.5 * math.log(10.0)))
    linear = (jnp.arange(NX)[:, None, None] * (NY * NZ) + jnp.arange(NY)[None, :, None] * NZ + jnp.arange(NZ)[None, None, :]).astype(jnp.float32) / (NX * NY * NZ - 1)
    amplitude = jnp.exp(0.5 * math.log(3.0) * linear)
    return matrix * row_scale * col_scale * amplitude[:, :, :, None, None, None]


def draw_keep_mask(key, part):
    drawn = jax.random.randint(key, (NX, NY, NZ, 7), 0, 4)
    keep = (drawn > 0).astype(jnp.int32)
    return keep.at[:, :, :, 0].set(1)


def setup_inputs(seed: int = 0) -> dict:
    arg_keys = jax.random.split(jax.random.key(seed), 3)
    hamiltonian = draw_hamiltonian(jax.random.fold_in(arg_keys[2], 71), 0)
    keep_mask = draw_keep_mask(jax.random.fold_in(arg_keys[2], 71), 0)
    return dict(hamiltonian=hamiltonian, keep_mask=keep_mask)


HIGHEST = lax.Precision.HIGHEST
OPPOSITE = (0, 2, 1, 4, 3, 6, 5)
TARGET_RMS = 1.0

def shifted(array, s):
    sign = 1 if s % 2 == 1 else -1
    return jnp.roll(array, -sign, (s - 1) // 2)

def block_mul(left, right):
    return jnp.einsum('xyzij,xyzjk->xyzik', left, right, precision=HIGHEST)

def product(left, right):
    left_self = left[:, :, :, 0]
    right_self = right[:, :, :, 0]
    centre = block_mul(left_self, right_self)
    others = []
    for s in range(1, 7):
        centre = centre + block_mul(left[:, :, :, s], shifted(right[:, :, :, OPPOSITE[s]], s))
        others.append(block_mul(left_self, right[:, :, :, s]) + block_mul(left[:, :, :, s], shifted(right_self, s)))
    return jnp.stack([centre] + others, axis=3)

def reference(hamiltonian, keep_mask):
    norm_sq = jnp.sum(hamiltonian * hamiltonian)
    factor = TARGET_RMS / jnp.sqrt(norm_sq / (NX * NY * NZ * B))
    iterate = factor * hamiltonian
    weights = keep_mask.astype(jnp.float32)[..., None, None]
    for sweep_index in range(ITERS):
        square = weights * product(iterate, iterate)
        cube = product(iterate, square)
        iterate = weights * (1.5 * iterate - 0.5 * cube)
    return iterate
```

```python
import jax
import jax.numpy as jnp
from jax import lax
from jax.sharding import PartitionSpec as P

TARGET_RMS = 1.0
AXES = ("gx", "gy", "gz")
SCALE = 2.0**30
KEEP_ROWS = 8


def passed_along(value, axis, steps):
    count = lax.axis_size(axis)
    pairs = [(source, (source + steps) % count) for source in range(count)]
    return lax.ppermute(value, axis, pairs)


def mul(spec, left, right):
    return jnp.einsum(spec, left, right, precision=lax.Precision.HIGH)


def summed_over(value, axis):
    count = lax.axis_size(axis)
    if count & (count - 1):
        return lax.psum(value, axis)
    step = 1
    while step < count:
        value = value + passed_along(value, axis, step)
        step *= 2
    return value


def from_sides(to_next, to_prev, axis):
    return passed_along(to_prev, axis, -1), passed_along(to_next, axis, 1)


def partners_along(blocks, slot, axis):
    if lax.axis_size(axis) == 2:
        both = passed_along(blocks[slot : slot + 2], axis, 1)
        return both[1], both[0]
    return from_sides(blocks[slot], blocks[slot + 1], axis)


def faces_along(block, axis):
    if lax.axis_size(axis) == 2:
        face = passed_along(block, axis, 1)
        return face, face
    return from_sides(block, block, axis)


def body(hamiltonian, keep_mask):
    raw = hamiltonian[0, 0, 0]
    keep = keep_mask[0, 0, 0].astype(jnp.float32)
    slots, width = raw.shape[0], raw.shape[-1]
    entry_count = width
    for axis in AXES:
        entry_count = entry_count * lax.axis_size(axis)
    blocks = raw * SCALE
    own = blocks[0]
    others = blocks[1:]

    partner_of = {}
    for axis, slot in (("gz", 5), ("gy", 3), ("gx", 1)):
        partner_of[slot], partner_of[slot + 1] = partners_along(blocks, slot, axis)
    partners = jnp.stack([partner_of[s] for s in range(1, slots)])

    keep_tile = jnp.zeros((KEEP_ROWS, width), jnp.float32).at[:slots, 0].set(keep)
    own_and_keep = jnp.concatenate([own, keep_tile], axis=0)
    face_of = {}
    for axis, slot in (("gz", 5), ("gy", 3), ("gx", 1)):
        face_of[slot], face_of[slot + 1] = faces_along(own_and_keep, axis)
    faces = jnp.stack([face_of[s][:width] for s in range(1, slots)])
    near_keep = jnp.stack(
        [face_of[s][width + (s + 1 if s % 2 else s - 1), 0] for s in range(1, slots)]
    )

    norm_sq = jnp.sum(raw * raw)
    for axis in AXES[::-1]:
        norm_sq = summed_over(norm_sq, axis)

    own_products = mul("ij,sjk->sik", own, blocks)
    side = mul("sij,sjk->sik", others, partners)
    square_own = own_products[0] + jnp.sum(side, axis=0)
    square_face_of = {}
    for axis, slot in (("gz", 5), ("gy", 3), ("gx", 1)):
        square_face_of[slot], square_face_of[slot + 1] = faces_along(square_own, axis)
    square_faces = jnp.stack([square_face_of[s] for s in range(1, slots)])

    near = near_keep[:, None, None]
    coupled = mul("sij,sjk->sik", others, faces)
    square_others = keep[1:, None, None] * (own_products[1:] + coupled)
    cube_own = (
        mul("ij,jk->ik", own, square_own)
        + mul("ij,jk->ik", jnp.sum(near * side, axis=0), own)
        + mul("sij,sjk->ik", near * coupled, partners)
    )
    cube_others = mul("ij,sjk->sik", own, square_others) + mul(
        "sij,sjk->sik", others, square_faces
    )
    cube = jnp.concatenate([cube_own[None], cube_others], axis=0)

    factor = TARGET_RMS / jnp.sqrt(norm_sq / entry_count)
    small = factor * (1.0 / SCALE)
    out = keep[:, None, None] * (
        1.5 * (factor * raw) - 0.5 * (((cube * small) * small) * small)
    )
    return out[None, None, None]


def solution(mesh):
    placed = (P("gx", "gy", "gz", None, None, None), P("gx", "gy", "gz", None))
    return jax.shard_map(
        body,
        mesh=mesh,
        in_specs=placed,
        out_specs=P("gx", "gy", "gz", None, None, None),
        check_vma=False,
    )
```

```python
import jax
import jax.numpy as jnp
from jax import lax
from jax.experimental import pallas as pl
from jax.experimental.pallas import tpu as pltpu
from jax.sharding import PartitionSpec as P

TARGET_RMS = 1.0
SIDES = (("gz", 5), ("gy", 3), ("gx", 1))
LOCAL_ORDER = (("gx", 1), ("gy", 3), ("gz", 5))
SCALE = 2.0**30
KEEP_ROWS = 8
WORD = jnp.float32
HALF = jnp.bfloat16
VMEM_BYTES = 16 * 2**20


def passed_along(value, axis, steps):
    count = lax.axis_size(axis)
    pairs = [(source, (source + steps) % count) for source in range(count)]
    return lax.ppermute(value, axis, pairs)


def partners_along(picked, axis):
    if lax.axis_size(axis) == 2:
        both = passed_along(picked[0], axis, 1)
        return (both, 1), (both, 0)
    return (
        (passed_along(picked[1], axis, -1), None),
        (passed_along(picked[0], axis, 1), None),
    )


def faces_along(block, axis):
    if lax.axis_size(axis) == 2:
        face = passed_along(block, axis, 1)
        return face, face
    return (passed_along(block, axis, -1), passed_along(block, axis, 1))


def summed_over(value, axis):
    total = value
    for step in range(1, lax.axis_size(axis)):
        total = total + passed_along(value, axis, step)
    return total


HBM = pl.BlockSpec(memory_space=pltpu.HBM)
VMEM = pl.BlockSpec(memory_space=pltpu.VMEM)
SMEM = pl.BlockSpec(memory_space=pltpu.SMEM)
PARAMS = pltpu.CompilerParams(vmem_limit_bytes=VMEM_BYTES)


def struct(*shape, dtype=WORD):
    return jax.ShapeDtypeStruct(shape, dtype)


def split(value):
    high = value.astype(HALF)
    return high, (value - high.astype(WORD)).astype(HALF)


def dot3(left, right):
    def dot(a, b):
        return jnp.dot(a, b, preferred_element_type=WORD)

    return dot(left[0], right[0]) + (dot(left[0], right[1]) + dot(left[1], right[0]))


def both(pair, s):
    return pair[0][s], pair[1][s]


def pick_pair(raw, slot, joined):
    width = raw.shape[-1]
    block = struct(width, width)
    shapes = [struct(2, width, width)] if joined else [block, block]

    def kernel(raw_ref, *rest):
        sem = rest[-1]
        copies = []
        for index, out in enumerate(rest[:-1]):
            source = raw_ref.at[pl.ds(slot, 2)] if joined else raw_ref.at[slot + index]
            copies.append(pltpu.make_async_copy(source, out, sem.at[index]))
        for copy in copies:
            copy.start()
        for copy in copies:
            copy.wait()

    return pl.pallas_call(
        kernel,
        in_specs=[HBM],
        out_specs=[VMEM] * len(shapes),
        out_shape=shapes,
        scratch_shapes=[pltpu.SemaphoreType.DMA((len(shapes),))],
        compiler_params=PARAMS,
    )(raw)


def pick_own(raw, keep):
    slots, width = raw.shape[0], raw.shape[-1]

    def kernel(raw_ref, keep_ref, out, sem):
        copy = pltpu.make_async_copy(raw_ref.at[0], out.at[pl.ds(0, width)], sem.at[0])
        copy.start()
        row = lax.broadcasted_iota(jnp.int32, (KEEP_ROWS, width), 0)
        tile = jnp.zeros((KEEP_ROWS, width), WORD)
        for s in range(slots):
            tile = jnp.where(row == s, keep_ref[s].astype(WORD), tile)
        out[pl.ds(width, KEEP_ROWS), :] = tile
        copy.wait()

    return pl.pallas_call(
        kernel,
        in_specs=[HBM, SMEM],
        out_specs=VMEM,
        out_shape=struct(width + KEEP_ROWS, width),
        scratch_shapes=[pltpu.SemaphoreType.DMA((1,))],
        compiler_params=PARAMS,
        name="pick_own",
    )(raw, keep)


def first_kernel(block_ref, high_ref, low_ref, product_ref, sum_ref, total):
    s = pl.program_id(0)
    raw = block_ref[0]
    half = split(raw * SCALE)
    high_ref[s], low_ref[s] = half

    @pl.when(s == 0)
    def _():
        total[...] = jnp.zeros_like(total)

    product_ref[s] = dot3((high_ref[0], low_ref[0]), half)
    rows = total.shape[0]
    total[...] += jnp.sum((raw * raw).reshape(-1, rows, raw.shape[-1]), axis=0)

    @pl.when(s == pl.num_programs(0) - 1)
    def _():
        sum_ref[0] = jnp.sum(total[...])


def first_products(raw):
    slots, width = raw.shape[0], raw.shape[-1]
    return pl.pallas_call(
        first_kernel,
        grid=(slots,),
        in_specs=[pl.BlockSpec((1, width, width), lambda s: (s, 0, 0))],
        out_specs=[VMEM, VMEM, VMEM, SMEM],
        out_shape=[
            struct(*raw.shape, dtype=HALF),
            struct(*raw.shape, dtype=HALF),
            struct(*raw.shape),
            struct(1),
        ],
        scratch_shapes=[pltpu.VMEM((8, width), WORD)],
        compiler_params=PARAMS,
        name="first_products",
    )(raw)


def side_products(halves, slot, partners, products=None, others=()):
    width = halves[0].shape[-1]
    operands = [*halves, partners[0][0], partners[1][0]]
    out_shape = [struct(2, width, width)]
    if products is not None:
        operands += [products, *others]
        out_shape.append(struct(width, width))

    def kernel(high, low, first, second, *rest):
        values = []
        for index, (ref, (_, part)) in enumerate(zip((first, second), partners)):
            value = ref[...] if part is None else ref[part]
            values.append(dot3(both((high, low), slot + index), split(value * SCALE)))
        if products is None:
            (side_ref,) = rest
        else:
            own, *sides, side_ref, square_ref = rest
            total = own[0]
            for other in sides:
                total = total + (other[0] + other[1])
            square_ref[...] = total + (values[0] + values[1])
        side_ref[0] = values[0]
        side_ref[1] = values[1]

    return pl.pallas_call(
        kernel,
        in_specs=[VMEM] * len(operands),
        out_specs=[VMEM] * len(out_shape),
        out_shape=out_shape,
        compiler_params=PARAMS,
    )(*operands)


def cube_parts(keep, halves, slot, faces, partners, products, side):
    width = halves[0].shape[-1]

    def kernel(keep_ref, high, low, f0, f1, p0, p1, products, side, pair, near, mix):
        nears, mixes = [], []
        for index, (face, ref, (_, part)) in enumerate(
            zip((f0, f1), (p0, p1), partners)
        ):
            s = slot + index
            back = width + slot + 1 - index
            kept = face[back : back + 1, :]
            value = ref[...] if part is None else ref[part]
            coupled = dot3(both((high, low), s), split(face[:width] * SCALE))
            square = keep_ref[s].astype(WORD) * (products[s] + coupled)
            pair[index] = dot3(both((high, low), 0), split(square))
            nears.append(dot3(split(kept * coupled), split(value * SCALE)))
            mixes.append(kept * side[index])
        near[...] = nears[0] + nears[1]
        mix[...] = mixes[0] + mixes[1]

    return pl.pallas_call(
        kernel,
        in_specs=[SMEM] + [VMEM] * 8,
        out_specs=[VMEM] * 3,
        out_shape=[
            struct(2, width, width),
            struct(width, width),
            struct(width, width),
        ],
        compiler_params=PARAMS,
    )(keep, *halves, *faces, partners[0][0], partners[1][0], products, side)


def own_cube(halves, square, parts):
    width = square.shape[-1]

    def kernel(high, low, square_ref, *rest):
        *refs, out = rest
        near, mix = refs[0][...], refs[1][...]
        for ref in refs[2::2]:
            near = near + ref[...]
        for ref in refs[3::2]:
            mix = mix + ref[...]
        own = both((high, low), 0)
        out[...] = dot3(own, split(square_ref[...])) + (dot3(split(mix), own) + near)

    return pl.pallas_call(
        kernel,
        in_specs=[VMEM] * (3 + len(parts)),
        out_specs=VMEM,
        out_shape=struct(width, width),
        compiler_params=PARAMS,
        name="own_cube",
    )(*halves, square, *parts)


def weighted(scalars, keep, raw, cube):
    small = scalars[1]
    kept = keep.astype(WORD)
    return kept * ((1.5 * scalars[0]) * raw - 0.5 * (((cube * small) * small) * small))


def own_output(scalars, keep, raw, cube):
    width = raw.shape[-1]
    block = pl.BlockSpec((1, width, width), lambda i: (0, 0, 0))

    def kernel(scalars, keep_ref, raw_ref, cube_ref, out):
        out[0] = weighted(scalars, keep_ref[0], raw_ref[0], cube_ref[...])

    return pl.pallas_call(
        kernel,
        grid=(1,),
        in_specs=[SMEM, SMEM, block, VMEM],
        out_specs=block,
        out_shape=struct(*raw.shape),
        compiler_params=PARAMS,
        name="own_output",
    )(scalars, keep, raw, cube)


def pair_output(scalars, keep, halves, raw, slot, square_faces, part, out):
    width = raw.shape[-1]
    block = pl.BlockSpec((1, width, width), lambda i: (slot + i, 0, 0))

    def kernel(scalars, keep_ref, high, low, raw_ref, f0, f1, part_ref, _, out_ref):
        for index, face in enumerate((f0, f1)):

            @pl.when(pl.program_id(0) == index)
            def _(index=index, face=face):
                s = slot + index
                cube = part_ref[index] + dot3(both((high, low), s), split(face[...]))
                out_ref[0] = weighted(scalars, keep_ref[s], raw_ref[0], cube)

    return pl.pallas_call(
        kernel,
        grid=(2,),
        in_specs=[SMEM, SMEM, VMEM, VMEM, block, VMEM, VMEM, VMEM, HBM],
        out_specs=block,
        out_shape=struct(*raw.shape),
        input_output_aliases={8: 0},
        compiler_params=PARAMS,
    )(scalars, keep, *halves, raw, *square_faces, part, out)


def body(hamiltonian, keep_mask):
    return step(hamiltonian[0, 0, 0], keep_mask[0, 0, 0])[None, None, None]


def step(raw, keep):
    entry_count = raw.shape[-1]
    for axis, _ in SIDES:
        entry_count = entry_count * lax.axis_size(axis)

    partners, faces, square_faces, side, parts = {}, {}, {}, {}, {}
    for axis, slot in SIDES:
        picked = pick_pair(raw, slot, lax.axis_size(axis) == 2)
        partners[slot] = partners_along(picked, axis)
    own = pick_own(raw, keep)
    for axis, slot in SIDES:
        faces[slot] = faces_along(own, axis)

    high, low, products, squares = first_products(raw)
    halves = (high, low)
    norm_sq = squares[0]
    for axis, _ in SIDES:
        norm_sq = summed_over(norm_sq, axis)
    factor = TARGET_RMS / jnp.sqrt(norm_sq / entry_count)
    scalars = jnp.stack([factor, factor * (1.0 / SCALE)])

    for axis, slot in LOCAL_ORDER[:-1]:
        (side[slot],) = side_products(halves, slot, partners[slot])
    slot = LOCAL_ORDER[-1][1]
    side[slot], square = side_products(
        halves, slot, partners[slot], products, tuple(side.values())
    )
    for axis, slot in SIDES:
        square_faces[slot] = faces_along(square, axis)

    sums = []
    for axis, slot in LOCAL_ORDER:
        parts[slot], near, mix = cube_parts(
            keep, halves, slot, faces[slot], partners[slot], products, side[slot]
        )
        sums += [near, mix]
    cube = own_cube(halves, square, sums)
    out = own_output(scalars, keep, raw, cube)
    for axis, slot in LOCAL_ORDER:
        out = pair_output(
            scalars, keep, halves, raw, slot, square_faces[slot], parts[slot], out
        )
    return out


def solution(mesh):
    placed = (P("gx", "gy", "gz", None, None, None), P("gx", "gy", "gz", None))
    return jax.shard_map(
        body,
        mesh=mesh,
        in_specs=placed,
        out_specs=P("gx", "gy", "gz", None, None, None),
        check_vma=False,
    )
```

```python
import jax
import jax.numpy as jnp
from jax import lax
from jax.experimental import pallas as pl
from jax.experimental.pallas import tpu as pltpu
from jax.sharding import PartitionSpec as P

TARGET_RMS = 1.0
SIDES = (("gz", 5), ("gy", 3), ("gx", 1))
LOCAL_ORDER = (("gx", 1), ("gy", 3), ("gz", 5))
SCALE = 2.0**30
KEEP_ROWS = 8
WORD = jnp.float32
HALF = jnp.bfloat16
VMEM_BYTES = 16 * 2**20


def passed_along(value, axis, steps):
    count = lax.axis_size(axis)
    pairs = [(source, (source + steps) % count) for source in range(count)]
    return lax.ppermute(value, axis, pairs)


def partners_along(picked, axis):
    if lax.axis_size(axis) == 2:
        both = passed_along(picked[0], axis, 1)
        return (both, 1), (both, 0)
    return (
        (passed_along(picked[1], axis, -1), None),
        (passed_along(picked[0], axis, 1), None),
    )


def faces_along(block, axis):
    if lax.axis_size(axis) == 2:
        face = passed_along(block, axis, 1)
        return face, face
    return (passed_along(block, axis, -1), passed_along(block, axis, 1))


def all_along(value, axis):
    steps = range(1, lax.axis_size(axis))
    return [value] + [passed_along(value, axis, k) for k in steps]


HBM = pl.BlockSpec(memory_space=pltpu.HBM)
VMEM = pl.BlockSpec(memory_space=pltpu.VMEM)
SMEM = pl.BlockSpec(memory_space=pltpu.SMEM)
PARAMS = pltpu.CompilerParams(vmem_limit_bytes=VMEM_BYTES)


def struct(*shape, dtype=WORD):
    return jax.ShapeDtypeStruct(shape, dtype)


def split(value):
    high = value.astype(HALF)
    return high, (value - high.astype(WORD)).astype(HALF)


def dot(left, right):
    return jnp.dot(left, right, preferred_element_type=WORD)


def beside(*values):
    return jnp.concatenate(values, axis=1)


def below(*values):
    return jnp.concatenate(values, axis=0)


def dot3(left, right):
    width = right[0].shape[1]
    wide = dot(left[0], beside(*right))
    return (wide[:, width:] + dot(left[1], right[0])) + wide[:, :width]


def dot3_sum(lefts, rights):
    left = [beside(*(pair[part] for pair in lefts)) for part in (0, 1)]
    right = [below(*(pair[part] for pair in rights)) for part in (0, 1)]
    return dot3(left, right)


def dot3_wide(left, rights):
    high, low = (beside(*(pair[part] for pair in rights)) for part in (0, 1))
    wide = dot(beside(*left), below(high, high)) + dot(left[0], low)
    width = wide.shape[1] // len(rights)
    return [wide[:, i * width : (i + 1) * width] for i in range(len(rights))]


def both(pair, s):
    return pair[0][s], pair[1][s]


def pick_pair(raw, slot, joined):
    width = raw.shape[-1]
    block = struct(width, width)
    shapes = [struct(2, width, width)] if joined else [block, block]

    def kernel(raw_ref, *rest):
        sem = rest[-1]
        copies = []
        for index, out in enumerate(rest[:-1]):
            source = raw_ref.at[pl.ds(slot, 2)] if joined else raw_ref.at[slot + index]
            copies.append(pltpu.make_async_copy(source, out, sem.at[index]))
        for copy in copies:
            copy.start()
        for copy in copies:
            copy.wait()

    return pl.pallas_call(
        kernel,
        in_specs=[HBM],
        out_specs=[VMEM] * len(shapes),
        out_shape=shapes,
        scratch_shapes=[pltpu.SemaphoreType.DMA((len(shapes),))],
        compiler_params=PARAMS,
    )(raw)


def pick_own(raw, keep):
    slots, width = raw.shape[0], raw.shape[-1]

    def kernel(raw_ref, keep_ref, out, sem):
        copy = pltpu.make_async_copy(raw_ref.at[0], out.at[pl.ds(0, width)], sem.at[0])
        copy.start()
        row = lax.broadcasted_iota(jnp.int32, (KEEP_ROWS, width), 0)
        tile = jnp.zeros((KEEP_ROWS, width), WORD)
        for s in range(slots):
            tile = jnp.where(row == s, keep_ref[s].astype(WORD), tile)
        out[pl.ds(width, KEEP_ROWS), :] = tile
        copy.wait()

    return pl.pallas_call(
        kernel,
        in_specs=[HBM, SMEM],
        out_specs=VMEM,
        out_shape=struct(width + KEEP_ROWS, width),
        scratch_shapes=[pltpu.SemaphoreType.DMA((1,))],
        compiler_params=PARAMS,
        name="pick_own",
    )(raw, keep)


def first_kernel(block_ref, high_ref, low_ref, product_ref, sum_ref, total):
    s = pl.program_id(0)
    raw = block_ref[0]
    half = split(raw * SCALE)
    high_ref[s], low_ref[s] = half

    @pl.when(s == 0)
    def _():
        total[...] = jnp.zeros_like(total)

    product_ref[s] = dot3((high_ref[0], low_ref[0]), half)
    rows = total.shape[0]
    total[...] += jnp.sum((raw * raw).reshape(-1, rows, raw.shape[-1]), axis=0)

    @pl.when(s == pl.num_programs(0) - 1)
    def _():
        sum_ref[0] = jnp.sum(total[...])


def first_products(raw):
    slots, width = raw.shape[0], raw.shape[-1]
    return pl.pallas_call(
        first_kernel,
        grid=(slots,),
        in_specs=[pl.BlockSpec((1, width, width), lambda s: (s, 0, 0))],
        out_specs=[VMEM, VMEM, VMEM, SMEM],
        out_shape=[
            struct(*raw.shape, dtype=HALF),
            struct(*raw.shape, dtype=HALF),
            struct(*raw.shape),
            struct(1),
        ],
        scratch_shapes=[pltpu.VMEM((8, width), WORD)],
        compiler_params=PARAMS,
        name="first_products",
    )(raw)


def side_products(halves, slot, partners, products=None, others=()):
    width = halves[0].shape[-1]
    operands = [*halves, partners[0][0], partners[1][0]]
    out_shape = [struct(2, width, width)]
    if products is not None:
        operands += [products, *others]
        out_shape.append(struct(width, width))

    def kernel(high, low, first, second, *rest):
        values = []
        for index, (ref, (_, part)) in enumerate(zip((first, second), partners)):
            value = ref[...] if part is None else ref[part]
            values.append(dot3(both((high, low), slot + index), split(value * SCALE)))
        if products is None:
            (side_ref,) = rest
        else:
            own, *sides, side_ref, square_ref = rest
            total = own[0]
            for other in sides:
                total = total + (other[0] + other[1])
            square_ref[...] = total + (values[0] + values[1])
        side_ref[0] = values[0]
        side_ref[1] = values[1]

    return pl.pallas_call(
        kernel,
        in_specs=[VMEM] * len(operands),
        out_specs=[VMEM] * len(out_shape),
        out_shape=out_shape,
        compiler_params=PARAMS,
    )(*operands)


def cube_parts(keep, halves, slot, faces, partners, products, side):
    width = halves[0].shape[-1]

    def kernel(keep_ref, high, low, f0, f1, p0, p1, products, side, pair, near, mix):
        squares, nears, values, mixes = [], [], [], []
        for index, (face, ref, (_, part)) in enumerate(
            zip((f0, f1), (p0, p1), partners)
        ):
            s = slot + index
            back = width + slot + 1 - index
            kept = face[back : back + 1, :]
            value = ref[...] if part is None else ref[part]
            coupled = dot3(both((high, low), s), split(face[:width] * SCALE))
            squares.append(split(keep_ref[s].astype(WORD) * (products[s] + coupled)))
            nears.append(split(kept * coupled))
            values.append(split(value * SCALE))
            mixes.append(kept * side[index])
        pair[0], pair[1] = dot3_wide(both((high, low), 0), squares)
        near[...] = dot3_sum(nears, values)
        mix[...] = mixes[0] + mixes[1]

    return pl.pallas_call(
        kernel,
        in_specs=[SMEM] + [VMEM] * 8,
        out_specs=[VMEM] * 3,
        out_shape=[
            struct(2, width, width),
            struct(width, width),
            struct(width, width),
        ],
        compiler_params=PARAMS,
    )(keep, *halves, *faces, partners[0][0], partners[1][0], products, side)


def own_cube(halves, square, parts):
    width = square.shape[-1]

    def kernel(high, low, square_ref, *rest):
        *refs, out = rest
        near, mix = refs[0][...], refs[1][...]
        for ref in refs[2::2]:
            near = near + ref[...]
        for ref in refs[3::2]:
            mix = mix + ref[...]
        own = both((high, low), 0)
        out[...] = near + dot3_sum((own, split(mix)), (split(square_ref[...]), own))

    return pl.pallas_call(
        kernel,
        in_specs=[VMEM] * (3 + len(parts)),
        out_specs=VMEM,
        out_shape=struct(width, width),
        compiler_params=PARAMS,
        name="own_cube",
    )(*halves, square, *parts)


def total_of(sums):
    def kernel(*refs):
        *parts, out = refs
        total = parts[0][0]
        for part in parts[1:]:
            total = total + part[0]
        out[0] = total

    return pl.pallas_call(
        kernel,
        in_specs=[SMEM] * len(sums),
        out_specs=SMEM,
        out_shape=struct(1),
        compiler_params=PARAMS,
        name="total_of",
    )(*sums)


def weighted(norm_refs, entry_count, keep, raw, cube):
    norm_sq = norm_refs[0][0]
    for ref in norm_refs[1:]:
        norm_sq = norm_sq + ref[0]
    row = jnp.full((1, raw.shape[-1]), norm_sq, WORD)
    factor = TARGET_RMS / jnp.sqrt(row / entry_count)
    small = factor * (1.0 / SCALE)
    kept = keep.astype(WORD)
    return kept * ((1.5 * factor) * raw - 0.5 * (((cube * small) * small) * small))


def own_output(norms, entry_count, keep, raw, cube):
    width = raw.shape[-1]
    block = pl.BlockSpec((1, width, width), lambda i: (0, 0, 0))
    count = len(norms)

    def kernel(*refs):
        keep_ref, raw_ref, cube_ref, out = refs[count:]
        out[0] = weighted(
            refs[:count], entry_count, keep_ref[0], raw_ref[0], cube_ref[...]
        )

    return pl.pallas_call(
        kernel,
        grid=(1,),
        in_specs=[SMEM] * count + [SMEM, block, VMEM],
        out_specs=block,
        out_shape=struct(*raw.shape),
        compiler_params=PARAMS,
        name="own_output",
    )(*norms, keep, raw, cube)


def pair_output(norms, entry_count, keep, halves, raw, slot, square_faces, part, out):
    width = raw.shape[-1]
    block = pl.BlockSpec((1, width, width), lambda i: (slot + i, 0, 0))
    count = len(norms)

    def kernel(*refs):
        keep_ref, high, low, raw_ref, f0, f1, part_ref, _, out_ref = refs[count:]
        for index, face in enumerate((f0, f1)):

            @pl.when(pl.program_id(0) == index)
            def _(index=index, face=face):
                s = slot + index
                cube = part_ref[index] + dot3(both((high, low), s), split(face[...]))
                out_ref[0] = weighted(
                    refs[:count], entry_count, keep_ref[s], raw_ref[0], cube
                )

    return pl.pallas_call(
        kernel,
        grid=(2,),
        in_specs=[SMEM] * count
        + [SMEM, VMEM, VMEM, block, VMEM, VMEM, VMEM, HBM],
        out_specs=block,
        out_shape=struct(*raw.shape),
        input_output_aliases={count + 7: 0},
        compiler_params=PARAMS,
    )(*norms, keep, *halves, raw, *square_faces, part, out)


def body(hamiltonian, keep_mask):
    return step(hamiltonian[0, 0, 0], keep_mask[0, 0, 0])[None, None, None]


def step(raw, keep):
    entry_count = raw.shape[-1]
    for axis, _ in SIDES:
        entry_count = entry_count * lax.axis_size(axis)

    partners, faces, square_faces, side, parts = {}, {}, {}, {}, {}
    for axis, slot in SIDES:
        picked = pick_pair(raw, slot, lax.axis_size(axis) == 2)
        partners[slot] = partners_along(picked, axis)
    own = pick_own(raw, keep)
    for axis, slot in SIDES:
        faces[slot] = faces_along(own, axis)

    high, low, products, squares = first_products(raw)
    halves = (high, low)
    norms = [squares]
    for axis, _ in SIDES:
        if len(norms) > 1:
            norms = [total_of(norms)]
        norms = all_along(norms[0], axis)

    for axis, slot in LOCAL_ORDER[:-1]:
        (side[slot],) = side_products(halves, slot, partners[slot])
    slot = LOCAL_ORDER[-1][1]
    side[slot], square = side_products(
        halves, slot, partners[slot], products, tuple(side.values())
    )
    for axis, slot in SIDES:
        square_faces[slot] = faces_along(square, axis)

    sums = []
    for axis, slot in LOCAL_ORDER:
        parts[slot], near, mix = cube_parts(
            keep, halves, slot, faces[slot], partners[slot], products, side[slot]
        )
        sums += [near, mix]
    cube = own_cube(halves, square, sums)
    out = own_output(norms, entry_count, keep, raw, cube)
    for axis, slot in LOCAL_ORDER:
        out = pair_output(
            norms,
            entry_count,
            keep,
            halves,
            raw,
            slot,
            square_faces[slot],
            parts[slot],
            out,
        )
    return out


def solution(mesh):
    placed = (P("gx", "gy", "gz", None, None, None), P("gx", "gy", "gz", None))
    return jax.shard_map(
        body,
        mesh=mesh,
        in_specs=placed,
        out_specs=P("gx", "gy", "gz", None, None, None),
        check_vma=False,
    )
```

```python
import jax
import jax.numpy as jnp
from jax import lax
from jax.experimental import pallas as pl
from jax.experimental.pallas import tpu as pltpu
from jax.sharding import PartitionSpec as P

TARGET_RMS = 1.0
SIDES = (("gz", 5), ("gy", 3), ("gx", 1))
LOCAL_ORDER = (("gx", 1), ("gy", 3), ("gz", 5))
SWAP_AXIS = "gz"
SCALE = 2.0**30
ROWS = 8
LANES = 128
WORD = jnp.float32
HALF = jnp.bfloat16
VMEM_BYTES = 16 * 2**20

HBM = pl.BlockSpec(memory_space=pltpu.HBM)
VMEM = pl.BlockSpec(memory_space=pltpu.VMEM)
SMEM = pl.BlockSpec(memory_space=pltpu.SMEM)
PARAMS = pltpu.CompilerParams(vmem_limit_bytes=VMEM_BYTES)


def swaps(axis):
    count = lax.axis_size(axis)
    return axis == SWAP_AXIS and count > 2 and count % 2 == 0


def way(axis, r):
    if swaps(axis):
        return (lax.axis_index(axis) + r) % 2
    return r


def passed_along(value, axis, steps):
    count = lax.axis_size(axis)
    pairs = [(source, (source + steps) % count) for source in range(count)]
    return lax.ppermute(value, axis, pairs)


def exchanged(outgoing, axis):
    count = lax.axis_size(axis)
    if swaps(axis):
        results = []
        for r in range(2):
            pairs = [(i, (i + 1 if (i + r) % 2 == 0 else i - 1) % count) for i in range(count)]
            results.append(lax.ppermute(outgoing[r], axis, pairs))
        return results
    return [passed_along(outgoing[1], axis, -1), passed_along(outgoing[0], axis, 1)]


def partners_along(picked, axis):
    if lax.axis_size(axis) == 2:
        joined = passed_along(picked[0][0], axis, 1)
        return [(joined, 1), (joined, 0)]
    return [(got, None) for got in exchanged([a for a, _ in picked], axis)]


def faces_along(block, axis):
    if lax.axis_size(axis) == 2:
        return [passed_along(block, axis, 1)] * 2
    return exchanged([block, block], axis)


def all_along(value, axis):
    steps = range(1, lax.axis_size(axis))
    return [value] + [passed_along(value, axis, k) for k in steps]


def struct(*shape, dtype=WORD):
    return jax.ShapeDtypeStruct(shape, dtype)


def split(value):
    high = value.astype(HALF)
    return high, (value - high.astype(WORD)).astype(HALF)


def dot(left, right):
    return jnp.dot(left, right, preferred_element_type=WORD)


def beside(*values):
    return jnp.concatenate(values, axis=1)


def below(*values):
    return jnp.concatenate(values, axis=0)


def dot3(left, right):
    width = right[0].shape[1]
    wide = dot(left[0], beside(*right))
    return (wide[:, width:] + dot(left[1], right[0])) + wide[:, :width]


def dot3_sum(lefts, rights):
    left = [beside(*(pair[part] for pair in lefts)) for part in (0, 1)]
    right = [below(*(pair[part] for pair in rights)) for part in (0, 1)]
    return dot3(left, right)


def dot3_wide(left, rights):
    high, low = (beside(*(pair[part] for pair in rights)) for part in (0, 1))
    wide = dot(beside(*left), below(high, high)) + dot(left[0], low)
    width = wide.shape[1] // len(rights)
    return [wide[:, i * width : (i + 1) * width] for i in range(len(rights))]


def both(pair, s):
    return pair[0][s], pair[1][s]


def read(ref, place):
    return ref[...] if place is None else ref[place]


def tiled(row, width):
    return beside(*[row] * (width // LANES))


def pick_pair(raw, axis, slot):
    width = raw.shape[-1]
    joined = lax.axis_size(axis) == 2
    block = struct(width, width)
    shapes = [struct(2, width, width)] if joined else [block, block]

    def kernel(raw_ref, *rest):
        *outs, sem = rest
        copies = []
        for r, out in enumerate(outs):
            source = raw_ref.at[pl.ds(slot, 2) if joined else slot + way(axis, r)]
            copies.append(pltpu.make_async_copy(source, out, sem.at[r]))
        for copy in copies:
            copy.start()
        for copy in copies:
            copy.wait()

    picked = pl.pallas_call(
        kernel,
        in_specs=[HBM],
        out_specs=[VMEM] * len(shapes),
        out_shape=shapes,
        scratch_shapes=[pltpu.SemaphoreType.DMA((len(shapes),))],
        compiler_params=PARAMS,
    )(raw)
    if joined:
        return [(picked[0], 0), (picked[0], 1)]
    return [(block, None) for block in picked]


def pick_own(raw, keep):
    slots, width = raw.shape[0], raw.shape[-1]

    def kernel(raw_ref, keep_ref, own, rows, own_and_rows, sem):
        targets = (own, own_and_rows.at[pl.ds(0, width)])
        copies = [
            pltpu.make_async_copy(raw_ref.at[0], target, sem.at[i])
            for i, target in enumerate(targets)
        ]
        for copy in copies:
            copy.start()
        row = lax.broadcasted_iota(jnp.int32, (ROWS, width), 0)
        tile = jnp.zeros((ROWS, width), WORD)
        for s in range(slots):
            tile = jnp.where(row == s, keep_ref[s].astype(WORD), tile)
        rows[...] = tile
        own_and_rows[pl.ds(width, ROWS), :] = tile
        for copy in copies:
            copy.wait()

    return pl.pallas_call(
        kernel,
        in_specs=[HBM, SMEM],
        out_specs=[VMEM] * 3,
        out_shape=[
            struct(width, width),
            struct(ROWS, width),
            struct(width + ROWS, width),
        ],
        scratch_shapes=[pltpu.SemaphoreType.DMA((2,))],
        compiler_params=PARAMS,
        name="pick_own",
    )(raw, keep)


def first_products(raw, keep_rows):
    slots, width = raw.shape[0], raw.shape[-1]

    def kernel(block_ref, keep_ref, high_ref, low_ref, product_ref, tile_ref, total):
        s = pl.program_id(0)
        block = block_ref[0]
        half = split(block * SCALE)
        high_ref[s], low_ref[s] = half

        @pl.when(s == 0)
        def _():
            total[...] = jnp.zeros_like(total)

        product_ref[s] = dot3((high_ref[0], low_ref[0]), half)
        total[...] += jnp.sum((block * block).reshape(-1, ROWS, width), axis=0)

        @pl.when(s == pl.num_programs(0) - 1)
        def _():
            row = lax.broadcasted_iota(jnp.int32, (ROWS, LANES), 0)
            norm = jnp.full((ROWS, LANES), jnp.sum(total[...]), WORD)
            tile_ref[...] = jnp.where(row == ROWS - 1, norm, keep_ref[:, :LANES])

    return pl.pallas_call(
        kernel,
        grid=(slots,),
        in_specs=[pl.BlockSpec((1, width, width), lambda s: (s, 0, 0)), VMEM],
        out_specs=[VMEM] * 4,
        out_shape=[
            struct(*raw.shape, dtype=HALF),
            struct(*raw.shape, dtype=HALF),
            struct(*raw.shape),
            struct(ROWS, LANES),
        ],
        scratch_shapes=[pltpu.VMEM((ROWS, width), WORD)],
        compiler_params=PARAMS,
        name="first_products",
    )(raw, keep_rows)


def side_products(halves, axis, slot, partners, products=None, others=()):
    width = halves[0].shape[-1]
    operands = [*halves, partners[0][0], partners[1][0]]
    out_shape = [struct(2, width, width)]
    if products is not None:
        operands += [products, *others]
        out_shape.append(struct(width, width))

    def kernel(high, low, first, second, *rest):
        values = []
        for r, (ref, (_, place)) in enumerate(zip((first, second), partners)):
            half = both((high, low), slot + way(axis, r))
            values.append(dot3(half, split(read(ref, place) * SCALE)))
        if products is None:
            (side_ref,) = rest
        else:
            own, *sides, side_ref, square_ref = rest
            total = own[0]
            for other in sides:
                total = total + (other[0] + other[1])
            square_ref[...] = total + (values[0] + values[1])
        side_ref[0] = values[0]
        side_ref[1] = values[1]

    return pl.pallas_call(
        kernel,
        in_specs=[VMEM] * len(operands),
        out_specs=[VMEM] * len(out_shape),
        out_shape=out_shape,
        compiler_params=PARAMS,
    )(*operands)


def cube_parts(keep_rows, halves, axis, slot, faces, nears, partners, products, side):
    width = halves[0].shape[-1]
    apart = nears is not None

    def kernel(keep, high, low, f0, f1, p0, p1, products, side, *rest):
        *tiles, pair, near, mix = rest
        squares, lefts, values, mixes = [], [], [], []
        for r, (face, ref, (_, place)) in enumerate(zip((f0, f1), (p0, p1), partners)):
            turn = way(axis, r)
            s = slot + turn
            back = slot + 1 - turn
            if not apart:
                near_keep = face[pl.ds(width + back, 1), :]
            elif isinstance(turn, int):
                near_keep = tiled(tiles[r][pl.ds(back, 1), :], width)
            else:
                here, there = (t[pl.ds(back, 1), :] for t in tiles)
                near_keep = tiled(jnp.where(turn == 0, here, there), width)
            coupled = dot3(both((high, low), s), split(face[:width] * SCALE))
            squares.append(split(keep[pl.ds(s, 1), :] * (products[s] + coupled)))
            lefts.append(split(near_keep * coupled))
            values.append(split(read(ref, place) * SCALE))
            mixes.append(near_keep * side[r])
        pair[0], pair[1] = dot3_wide(both((high, low), 0), squares)
        near[...] = dot3_sum(lefts, values)
        mix[...] = mixes[0] + mixes[1]

    operands = [keep_rows, *halves, *faces, partners[0][0], partners[1][0]]
    operands += [products, side, *(nears or ())]
    return pl.pallas_call(
        kernel,
        in_specs=[VMEM] * len(operands),
        out_specs=[VMEM] * 3,
        out_shape=[
            struct(2, width, width),
            struct(width, width),
            struct(width, width),
        ],
        compiler_params=PARAMS,
    )(*operands)


def own_cube(halves, square, parts):
    width = square.shape[-1]

    def kernel(high, low, square_ref, *rest):
        *refs, out = rest
        near, mix = refs[0][...], refs[1][...]
        for ref in refs[2::2]:
            near = near + ref[...]
        for ref in refs[3::2]:
            mix = mix + ref[...]
        own = both((high, low), 0)
        out[...] = near + dot3_sum((own, split(mix)), (split(square_ref[...]), own))

    return pl.pallas_call(
        kernel,
        in_specs=[VMEM] * (3 + len(parts)),
        out_specs=VMEM,
        out_shape=struct(width, width),
        compiler_params=PARAMS,
        name="own_cube",
    )(*halves, square, *parts)


def total_of(tiles):
    def kernel(*refs):
        *parts, out = refs
        total = parts[0][...]
        for part in parts[1:]:
            total = total + part[...]
        out[...] = total

    return pl.pallas_call(
        kernel,
        in_specs=[VMEM] * len(tiles),
        out_specs=VMEM,
        out_shape=struct(ROWS, LANES),
        compiler_params=PARAMS,
        name="total_of",
    )(*tiles)


def outputs_of(
    norms, entry_count, keep_rows, halves, axis, slot, raws, faces, part, own=None, out=None
):
    width = part.shape[-1]
    shape = halves[0].shape
    count = len(norms)
    chunk = width // 2

    def kernel(*refs):
        norm_refs, rest = refs[:count], refs[count:]
        keep, high, low, raw0, raw1, f0, f1, part_ref, *rest = rest
        *given, out_ref, staged, sem = rest
        norm_sq = norm_refs[0][ROWS - 1 :, :]
        for ref in norm_refs[1:]:
            norm_sq = norm_sq + ref[ROWS - 1 :, :]
        factor = tiled(TARGET_RMS / jnp.sqrt(norm_sq / entry_count), width)
        small = factor * (1.0 / SCALE)
        copies = []

        def put(place, s, rows, raw, cube):
            kept = keep[pl.ds(s, 1), :]
            staged[place, rows, :] = kept * (
                (1.5 * factor) * raw - 0.5 * (((cube * small) * small) * small)
            )
            copy = pltpu.make_async_copy(
                staged.at[place, rows],
                out_ref.at[s, rows],
                sem.at[len(copies)],
            )
            copy.start()
            copies.append(copy)

        if own is not None:
            own_ref, cube_ref = given
            put(2, 0, pl.ds(0, width), own_ref[...], cube_ref[...])
        for r, (raw_ref, face) in enumerate(((raw0, f0), (raw1, f1))):
            s = slot + way(axis, r)
            right = split(face[...])
            for start in range(0, width, chunk):
                rows = pl.ds(start, chunk)
                left = (high[s, rows, :], low[s, rows, :])
                cube = part_ref[r, rows, :] + dot3(left, right)
                place = raws[r][1]
                raw = raw_ref[rows, :] if place is None else raw_ref[place, rows, :]
                put(r, s, rows, raw, cube)
        for copy in copies:
            copy.wait()

    operands = [*norms, keep_rows, *halves, raws[0][0], raws[1][0], *faces, part]
    operands += own if own is not None else []
    in_specs = [VMEM] * len(operands)
    aliases = {}
    if out is not None:
        aliases = {len(operands): 0}
        operands.append(out)
        in_specs.append(HBM)
    return pl.pallas_call(
        kernel,
        in_specs=in_specs,
        out_specs=HBM,
        out_shape=struct(*shape),
        scratch_shapes=[
            pltpu.VMEM((3, width, width), WORD),
            pltpu.SemaphoreType.DMA((5,)),
        ],
        input_output_aliases=aliases,
        compiler_params=PARAMS,
    )(*operands)


def body(hamiltonian, keep_mask):
    return step(hamiltonian[0, 0, 0], keep_mask[0, 0, 0])[None, None, None]


def step(raw, keep):
    raw = pltpu.with_memory_space_constraint(raw, pltpu.HBM)
    entry_count = raw.shape[-1]
    for axis, _ in SIDES:
        entry_count = entry_count * lax.axis_size(axis)

    picked, partners, faces, nears, square_faces, side, parts = ({} for _ in range(7))
    for axis, slot in SIDES:
        picked[slot] = pick_pair(raw, axis, slot)
        partners[slot] = partners_along(picked[slot], axis)
    own, keep_rows, own_and_rows = pick_own(raw, keep)
    high, low, products, tile = first_products(raw, keep_rows)
    halves = (high, low)

    norms = [tile]
    for axis, slot in SIDES:
        if len(norms) > 1:
            norms = [total_of(norms)]
        norms = all_along(norms[0], axis)
        if axis == SWAP_AXIS:
            nears[slot] = [norms[-1], norms[1]]
    for axis, slot in SIDES:
        payload = own_and_rows if slot not in nears else own
        faces[slot] = faces_along(payload, axis)

    for axis, slot in LOCAL_ORDER[:-1]:
        (side[slot],) = side_products(halves, axis, slot, partners[slot])
    axis, slot = LOCAL_ORDER[-1]
    side[slot], square = side_products(
        halves, axis, slot, partners[slot], products, tuple(side.values())
    )
    for axis, slot in SIDES:
        square_faces[slot] = faces_along(square, axis)

    sums = []
    for axis, slot in LOCAL_ORDER:
        parts[slot], near, mix = cube_parts(
            keep_rows,
            halves,
            axis,
            slot,
            faces[slot],
            nears.get(slot),
            partners[slot],
            products,
            side[slot],
        )
        sums += [near, mix]
    cube = own_cube(halves, square, sums)

    out = None
    for axis, slot in LOCAL_ORDER:
        out = outputs_of(
            norms,
            entry_count,
            keep_rows,
            halves,
            axis,
            slot,
            picked[slot],
            square_faces[slot],
            parts[slot],
            own=[own, cube] if out is None else None,
            out=out,
        )
    return out


def solution(mesh):
    placed = (P("gx", "gy", "gz", None, None, None), P("gx", "gy", "gz", None))
    return jax.shard_map(
        body,
        mesh=mesh,
        in_specs=placed,
        out_specs=P("gx", "gy", "gz", None, None, None),
        check_vma=False,
    )
```
